256 devices in a mesh: row: 32 (over y, z), col: 8 (over x, core).
Axes of the slice: x: 4, y: 4, z: 8, core: 2. Of those that a mesh axis runs over, the one named last changes fastest.
Arguments:
- acts: bfloat16 [6144, 28672], P('col', 'row'), may hold values from -12 to 12
- out_grad: bfloat16 [6144, 8192], P('row', 'col'), may hold values from -12 to 12
- lengths: int32 [8], replicated, may hold values from 1 to 768, 4800 in all
Outputs:
- weight_grad: bfloat16 [28672, 8192], P('row', 'col')
- norms: float32 [8], replicated
The draws below stay inside these ranges and needn't reach their ends.
All inputs are finite; a program needn't handle non-finite values.
Results may differ from the reference program's by a relative error of at most 0.0013.
Values may be sent and summed in bfloat16 or wider, within the bound.
No kernel may reach another device: no remote copies, remote signals or barrier semaphores. Data moves between devices by JAX's collectives and lax.ppermute only.
A program may use at most 128 MiB of HBM per device.

```python
import math
import jax
import jax.numpy as jnp
import numpy as np
from jax import lax

FF = 28672
D = 8192
SEQS = 8
LEN = 768
TOKENS = 6144


shared_count = 8


shared_weight = 0.2


def shared_coeffs(key):
    base = jax.random.fold_in(key, 101)
    scales = jax.random.uniform(jax.random.fold_in(base, 1), (SEQS, shared_count), jnp.float32, 0.4, 1.6)
    coeffs = jax.random.normal(jax.random.fold_in(base, 2), (TOKENS, shared_count), jnp.float32)
    return coeffs * jnp.repeat(scales, LEN, axis=0)


def with_shared(random_part, coeffs, directions):
    total = random_part
    for index in range(shared_count):
        total = total + shared_weight * coeffs[:, index:index + 1] * directions[index][None, :]
    return total


def draw_acts(key, part):
    coeffs = shared_coeffs(key)
    directions = jax.random.normal(jax.random.fold_in(key, 211), (shared_count, FF), jnp.float32)
    random_part = jax.random.normal(jax.random.fold_in(key, 212), (TOKENS, FF), jnp.float32)
    ramp = jnp.arange(FF, dtype=jnp.float32) / jnp.float32(FF - 1)
    rough = jax.random.uniform(jax.random.fold_in(key, 213), (FF,), jnp.float32, 0.7, 1.3)
    feature_scale = jnp.exp(ramp * jnp.log(jnp.float32(3.0))) * rough
    total = with_shared(random_part, coeffs, directions) * feature_scale[None, :]
    return jnp.clip(total, -12.0, 12.0).astype(jnp.bfloat16)


def draw_out_grad(key, part):
    coeffs = shared_coeffs(key)
    directions = jax.random.normal(jax.random.fold_in(key, 311), (shared_count, D), jnp.float32)
    random_part = jax.random.normal(jax.random.fold_in(key, 312), (TOKENS, D), jnp.float32)
    return jnp.clip(with_shared(random_part, coeffs, directions), -12.0, 12.0).astype(jnp.bfloat16)


def length_profile(amount, total, reach, skew):
    weights = [(1 << 20) // math.isqrt(rank ** skew) + 1 for rank in range(2, amount + 1)]
    spare, counts = total - reach - (amount - 1), [1] * (amount - 1)
    while spare > 0:
        candidates = [i for i in range(amount - 1) if counts[i] < reach]
        mass, remaining = sum([weights[i] for i in candidates]), spare
        for i in candidates:
            extra = min(reach - counts[i], max(1, remaining * weights[i] // mass), spare)
            counts[i] = counts[i] + extra
            spare = spare - extra
    return np.array([reach] + counts)


def ragged_sizes(rng, number_of, total, bound, slope):
    if number_of == 2:
        one = jax.random.randint(rng, (), max(1, total - bound), min(bound, total - 1) + 1)
        return jnp.stack([one, total - one])
    sizes = jnp.asarray(length_profile(number_of, total, bound, slope), jnp.int32)
    couples = (number_of - 1) // 2
    giver, receiver = sizes[1:1 + 2 * couples:2], sizes[2:2 + 2 * couples:2]
    slack = jnp.minimum(giver - 1, bound - receiver)
    shifted = jax.random.randint(jax.random.fold_in(rng, 1), (couples,), 0, 1 << 20) % (slack + 1)
    sizes = sizes.at[1:1 + 2 * couples:2].set(giver - shifted).at[2:2 + 2 * couples:2].set(receiver + shifted)
    return sizes[jax.random.permutation(jax.random.fold_in(rng, 2), number_of)]


def setup_inputs(seed: int = 0) -> dict:
    key_list = jax.random.split(jax.random.key(seed), 4)
    acts = draw_acts(jax.random.fold_in(key_list[3], 71), 0)
    out_grad = draw_out_grad(jax.random.fold_in(key_list[3], 71), 0)
    lengths = ragged_sizes(key_list[2], SEQS, SEQS * LEN - (SEQS - 1) * (LEN // 4), LEN, 0).astype(jnp.int32)
    return {"acts": acts, "out_grad": out_grad, "lengths": lengths}


def reference(acts, out_grad, lengths):
    positions = jnp.arange(TOKENS, dtype=jnp.int32)
    seq_of = positions // LEN
    limit = lax.optimization_barrier(jnp.sum(jnp.where(seq_of[:, None] == jnp.arange(SEQS, dtype=jnp.int32)[None, :], lengths[None, :], 0), axis=1))
    live = positions % LEN < limit
    grads = jnp.where(live[:, None], out_grad, jnp.zeros_like(out_grad))
    divisor = float(FF) * float(D) * float(LEN)
    norm_list = []
    for seq in range(SEQS):
        act_rows = acts[seq * LEN:(seq + 1) * LEN]
        grad_rows = grads[seq * LEN:(seq + 1) * LEN]
        act_gram = jnp.dot(act_rows, act_rows.T, preferred_element_type=jnp.float32)
        grad_gram = jnp.dot(grad_rows, grad_rows.T, preferred_element_type=jnp.float32)
        squares = jnp.sum(act_gram * grad_gram)
        norm_list.append(jnp.sqrt(squares / divisor))
    norms = jnp.stack(norm_list).astype(jnp.float32)
    scale = 1.0 / (norms + 0.1)
    total = jnp.zeros((FF, D), jnp.float32)
    for seq in range(SEQS):
        act_rows = acts[seq * LEN:(seq + 1) * LEN]
        grad_rows = grads[seq * LEN:(seq + 1) * LEN]
        total = total + scale[seq] * jnp.dot(act_rows.T, grad_rows, preferred_element_type=jnp.float32)
    weight_grad = (total / jnp.sqrt(jnp.float32(TOKENS))).astype(jnp.bfloat16)
    return (weight_grad, norms)
```

```python
import jax
import jax.numpy as jnp
from jax import lax
from jax.sharding import PartitionSpec as P

FF = 28672
D = 8192


def body(acts, out_grad, lengths):
    n_row = lax.axis_size("row")
    own_rows = out_grad.shape[0]
    tokens = own_rows * n_row
    seqs = lengths.shape[0]
    seq_len = tokens // seqs
    slot = lax.broadcasted_iota(jnp.int32, (seq_len, 1), 0)
    act_full = lax.all_gather(acts, "col", axis=0, tiled=True)
    grad_full = lax.all_gather(out_grad, "row", axis=0, tiled=True)
    products = []
    locals_ = []
    for seq in range(seqs):
        act_rows = act_full[seq * seq_len : (seq + 1) * seq_len]
        grad_rows = grad_full[seq * seq_len : (seq + 1) * seq_len]
        grad_rows = jnp.where(slot < lengths[seq], grad_rows, jnp.zeros_like(grad_rows))
        product = lax.dot_general(
            act_rows, grad_rows, (((0,), (0,)), ((), ())), preferred_element_type=jnp.float32
        )
        products.append(product)
        locals_.append(jnp.sum(product * product))
    squares = lax.psum(jnp.stack(locals_), ("row", "col"))
    divisor = float(FF) * float(D) * float(seq_len)
    norms = jnp.sqrt(squares / divisor)
    scale = 1.0 / (norms + 0.1)
    total = scale[0] * products[0]
    for seq in range(1, seqs):
        total = total + scale[seq] * products[seq]
    weight_grad = (total / jnp.sqrt(jnp.float32(tokens))).astype(jnp.bfloat16)
    return (weight_grad, norms)


def solution(mesh):
    placed = (P("col", "row"), P("row", "col"), P())
    return jax.shard_map(
        body, mesh=mesh, in_specs=placed, out_specs=(P("row", "col"), P()), check_vma=False
    )
```

```python
import math

import jax
import jax.numpy as jnp
from jax import lax
from jax.experimental import pallas as pl
from jax.experimental.pallas import tpu as pltpu
from jax.sharding import PartitionSpec as P

FF = 28672
D = 8192
SEQS = 8
LEN = 768
NY = 4
NZ = 8
OWN = SEQS * LEN // (NY * NZ)
ORDER = (0, 1, 3, 2)


def z_shift(value, step):
    pairs = [(i, i // NZ * NZ + (i % NZ + step) % NZ) for i in range(NY * NZ)]
    return lax.ppermute(value, "row", pairs)


def y_shift(value, step):
    pairs = [(i, (i + NZ * step) % (NY * NZ)) for i in range(NY * NZ)]
    return lax.ppermute(value, "row", pairs)


def z_ring(own):
    half = own.shape[0] // 2
    up1, down1 = z_shift(own, 1), z_shift(own, -1)
    up2, down2 = z_shift(up1, 1), z_shift(down1, -1)
    up3, down3 = z_shift(up2, 1), z_shift(down2, -1)
    up4, down4 = z_shift(up3[:half], 1), z_shift(down3[half:], -1)
    return [own, down1, down2, down3, up4, down4, up3, up2, up1]


def y_ring(own):
    half = own.shape[0] // 2
    up1, down1 = y_shift(own, 1), y_shift(own, -1)
    up2, down2 = y_shift(up1[:half], 1), y_shift(down1[half:], -1)
    return [own, down1, up2, down2, up1]


def products_kernel(*refs):
    acts, left, right = refs[0], refs[1:6], refs[6:15]
    prod, squares, grads, act_buf, grad_sem, act_sem = refs[15:]
    row = lax.axis_index("row")
    y, z = row // NZ, row % NZ
    width = left[0].shape[1]

    def left_source(rel, k):
        if rel == 2:
            return left[2 + k // 4].at[pl.ds(k % 4 * OWN, OWN)]
        return left[{0: 0, 1: 1, 3: 4}[rel]].at[pl.ds(k * OWN, OWN)]

    def right_source(rel, k):
        if k == 4:
            return right[4 + rel // 2].at[pl.ds(rel % 2 * OWN, OWN)]
        return right[k if k < 4 else k + 1].at[pl.ds(rel * OWN, OWN)]

    def seq_of(i):
        pair = i // 2
        rel = jnp.where(pair == 2, 3, jnp.where(pair == 3, 2, pair))
        return 2 * ((y + rel) % NY) + i % 2

    def act_copy(i):
        start = pl.multiple_of(seq_of(i) * LEN, LEN)
        return pltpu.make_async_copy(acts.at[pl.ds(start, LEN)], act_buf.at[i % 2], act_sem.at[i % 2])

    act_copy(0).start()
    for place, rel in enumerate(ORDER):
        for k in range(NZ):
            owner = (z + k) % NZ
            slot = 2 * place + owner // 4
            rows = pl.ds(pl.multiple_of(owner % 4 * OWN, OWN), OWN)
            sem = grad_sem.at[place]
            pltpu.make_async_copy(left_source(rel, k), grads.at[slot, rows, pl.ds(0, width)], sem).start()
            pltpu.make_async_copy(right_source(rel, k), grads.at[slot, rows, pl.ds(width, width)], sem).start()

    lane = lax.broadcasted_iota(jnp.int32, squares.shape, 1)

    def step(i, acc):
        @pl.when(i + 1 < SEQS)
        def _():
            act_copy(i + 1).start()

        @pl.when(i % 2 == 0)
        def _():
            both = grads.at[pl.ds(pl.multiple_of(i, 2), 2)]
            pltpu.make_async_copy(both, both, grad_sem.at[i // 2]).wait()

        act_copy(i).wait()
        p = lax.dot_general(
            act_buf[i % 2], grads[i], (((0,), (0,)), ((), ())), preferred_element_type=jnp.float32
        )
        prod[i] = p
        return jnp.where(lane == seq_of(i), jnp.sum(p * p), acc)

    squares[...] = lax.fori_loop(0, SEQS, step, jnp.zeros(squares.shape, jnp.float32))


def combine_kernel(parts, prod, out, norms, out_buf, sem):
    row = lax.axis_index("row")
    y = row // NZ
    squares = jnp.sum(parts[...], axis=0, keepdims=True)
    norm = jnp.sqrt(squares / (float(FF) * float(D) * float(LEN)))
    norms[...] = norm
    scale = (1.0 / (norm + 0.1)) / math.sqrt(SEQS * LEN)
    lane = lax.broadcasted_iota(jnp.int32, scale.shape, 1)
    factors = []
    for i in range(SEQS):
        seq = 2 * ((y + ORDER[i // 2]) % NY) + i % 2
        factors.append(jnp.sum(jnp.where(lane == seq, scale, 0.0)))
    rows = 128
    chunks = out.shape[0] // rows

    def copy(c):
        at = pl.ds(pl.multiple_of(c * rows, rows), rows)
        return pltpu.make_async_copy(out_buf.at[at], out.at[at], sem.at[c])

    def step(c, carry):
        at = pl.ds(pl.multiple_of(c * rows, rows), rows)
        total = factors[0] * prod[0, at]
        for i in range(1, SEQS):
            total = total + factors[i] * prod[i, at]
        out_buf[at] = total.astype(jnp.bfloat16)
        copy(c).start()
        return carry

    lax.fori_loop(0, chunks, step, 0)
    for c in range(chunks):
        copy(c).wait()


def body(acts, out_grad, lengths):
    row = lax.axis_index("row")
    feats, width = acts.shape[1], out_grad.shape[1]
    devices = lax.axis_size("row") * lax.axis_size("col")
    act_full = lax.all_gather(acts, "col", axis=0, tiled=True)

    first = row * OWN
    slot = first % LEN + lax.broadcasted_iota(jnp.int32, (OWN, 1), 0)
    own = jnp.where(slot < lengths[first // LEN], out_grad, jnp.zeros_like(out_grad))
    left = z_ring(own[:, : width // 2])
    right = y_ring(own[:, width // 2 :])
    left = y_ring(jnp.concatenate(left, axis=0))
    right = z_ring(jnp.concatenate(right, axis=0))

    anywhere = pl.BlockSpec(memory_space=pl.ANY)
    vmem = pl.BlockSpec(memory_space=pltpu.VMEM)
    prod, squares = pl.pallas_call(
        products_kernel,
        out_shape=(
            pltpu.VMEM((SEQS, feats, width), jnp.float32),
            jax.ShapeDtypeStruct((devices, SEQS), jnp.float32),
        ),
        in_specs=[anywhere] * 15,
        out_specs=(vmem, vmem),
        scratch_shapes=[
            pltpu.VMEM((SEQS, LEN, width), jnp.bfloat16),
            pltpu.VMEM((2, LEN, feats), jnp.bfloat16),
            pltpu.SemaphoreType.DMA((NY,)),
            pltpu.SemaphoreType.DMA((2,)),
        ],
        compiler_params=pltpu.CompilerParams(vmem_limit_bytes=26 << 20),
        name="sequence_products",
    )(act_full, *left, *right)
    parts = lax.all_to_all(squares, ("row", "col"), 0, 0, tiled=True)
    weight_grad, norms = pl.pallas_call(
        combine_kernel,
        out_shape=(
            jax.ShapeDtypeStruct((feats, width), jnp.bfloat16),
            jax.ShapeDtypeStruct((1, SEQS), jnp.float32),
        ),
        in_specs=[vmem, vmem],
        out_specs=(anywhere, vmem),
        scratch_shapes=[
            pltpu.VMEM((feats, width), jnp.bfloat16),
            pltpu.SemaphoreType.DMA((feats // 128,)),
        ],
        compiler_params=pltpu.CompilerParams(vmem_limit_bytes=16 << 20),
        name="scaled_sum",
    )(parts, prod)
    return (weight_grad, norms.reshape(SEQS))


def solution(mesh):
    placed = (P("col", "row"), P("row", "col"), P())
    return jax.shard_map(
        body, mesh=mesh, in_specs=placed, out_specs=(P("row", "col"), P()), check_vma=False
    )
```

```python
import functools
import math

import jax
import jax.numpy as jnp
from jax import lax
from jax.experimental import pallas as pl
from jax.experimental.pallas import tpu as pltpu
from jax.sharding import PartitionSpec as P

FF = 28672
D = 8192
SEQS = 8
LEN = 768
NY = 4
NZ = 8
OWN = SEQS * LEN // (NY * NZ)
SENT = 3
ORDER = (0, 1, 3, 2)


def z_shift(value, step):
    pairs = [(i, i // NZ * NZ + (i % NZ + step) % NZ) for i in range(NY * NZ)]
    return lax.ppermute(value, "row", pairs)


def y_shift(value, step):
    pairs = [(i, (i + NZ * step) % (NY * NZ)) for i in range(NY * NZ)]
    return lax.ppermute(value, "row", pairs)


def z_ring(own):
    half = own.shape[0] // 2
    up1, down1 = z_shift(own, 1), z_shift(own, -1)
    up2, down2 = z_shift(up1, 1), z_shift(down1, -1)
    up3, down3 = z_shift(up2, 1), z_shift(down2, -1)
    up4, down4 = z_shift(up3[:half], 1), z_shift(down3[half:], -1)
    return [own, down1, down2, down3, up4, down4, up3, up2, up1]


def y_ring(own):
    half = own.shape[0] // 2
    up1, down1 = y_shift(own, 1), y_shift(own, -1)
    up2, down2 = y_shift(up1[:half], 1), y_shift(down1[half:], -1)
    return [own, down1, up2, down2, up1]


def products_kernel(*refs):
    acts, left, right = refs[0], refs[1:6], refs[6:15]
    kept, sent, squares, grads, act_buf, stage, grad_sem, act_sem, sent_sem = refs[15:]
    row = lax.axis_index("row")
    y, z = row // NZ, row % NZ
    width = left[0].shape[1]

    def left_source(rel, k):
        if rel == 2:
            return left[2 + k // 4].at[pl.ds(k % 4 * OWN, OWN)]
        return left[{0: 0, 1: 1, 3: 4}[rel]].at[pl.ds(k * OWN, OWN)]

    def right_source(rel, k):
        if k == 4:
            return right[4 + rel // 2].at[pl.ds(rel % 2 * OWN, OWN)]
        return right[k if k < 4 else k + 1].at[pl.ds(rel * OWN, OWN)]

    def seq_of(i):
        pair = i // 2
        rel = jnp.where(pair == 2, 3, jnp.where(pair == 3, 2, pair))
        return 2 * ((y + rel) % NY) + i % 2

    def act_copy(i):
        start = pl.multiple_of(seq_of(i) * LEN, LEN)
        return pltpu.make_async_copy(acts.at[pl.ds(start, LEN)], act_buf.at[i % 2], act_sem.at[i % 2])

    act_copy(0).start()
    for place, rel in enumerate(ORDER):
        for k in range(NZ):
            owner = (z + k) % NZ
            slot = 2 * place + owner // 4
            rows = pl.ds(pl.multiple_of(owner % 4 * OWN, OWN), OWN)
            sem = grad_sem.at[place]
            pltpu.make_async_copy(left_source(rel, k), grads.at[slot, rows, pl.ds(0, width)], sem).start()
            pltpu.make_async_copy(right_source(rel, k), grads.at[slot, rows, pl.ds(width, width)], sem).start()

    lane = lax.broadcasted_iota(jnp.int32, squares.shape, 1)

    def sent_copy(i):
        return pltpu.make_async_copy(stage.at[i], sent.at[i], sent_sem.at[i])

    def step(to_hbm, i, acc):
        @pl.when(i + 1 < SEQS)
        def _():
            act_copy(i + 1).start()

        @pl.when(i % 2 == 0)
        def _():
            both = grads.at[pl.ds(pl.multiple_of(i, 2), 2)]
            pltpu.make_async_copy(both, both, grad_sem.at[i // 2]).wait()

        act_copy(i).wait()
        p = lax.dot_general(
            act_buf[i % 2], grads[i], (((0,), (0,)), ((), ())), preferred_element_type=jnp.float32
        )
        if to_hbm:
            stage[i] = p
            sent_copy(i).start()
        else:
            kept[i - SENT] = p
        return jnp.where(lane == seq_of(i), jnp.sum(p * p), acc)

    acc = jnp.zeros(squares.shape, jnp.float32)
    acc = lax.fori_loop(0, SENT, functools.partial(step, True), acc)
    squares[...] = lax.fori_loop(SENT, SEQS, functools.partial(step, False), acc)
    for i in range(SENT):
        sent_copy(i).wait()


def combine_kernel(parts, kept, sent, out, norms, out_buf, back, sem, back_sem):
    rows = 128
    chunks = out.shape[0] // rows

    def back_copy(c):
        at = pl.ds(pl.multiple_of(c * rows, rows), rows)
        return pltpu.make_async_copy(sent.at[pl.ds(0, SENT), at], back.at[:, at], back_sem.at[c])

    for c in range(chunks):
        back_copy(c).start()
    row = lax.axis_index("row")
    y = row // NZ
    squares = jnp.sum(parts[...], axis=0, keepdims=True)
    norm = jnp.sqrt(squares / (float(FF) * float(D) * float(LEN)))
    norms[...] = norm
    scale = (1.0 / (norm + 0.1)) / math.sqrt(SEQS * LEN)
    lane = lax.broadcasted_iota(jnp.int32, scale.shape, 1)
    factors = []
    for i in range(SEQS):
        seq = 2 * ((y + ORDER[i // 2]) % NY) + i % 2
        factors.append(jnp.sum(jnp.where(lane == seq, scale, 0.0)))

    def copy(c):
        at = pl.ds(pl.multiple_of(c * rows, rows), rows)
        return pltpu.make_async_copy(out_buf.at[at], out.at[at], sem.at[c])

    def step(c, carry):
        at = pl.ds(pl.multiple_of(c * rows, rows), rows)
        back_copy(c).wait()
        total = factors[0] * back[0, at]
        for i in range(1, SENT):
            total = total + factors[i] * back[i, at]
        for i in range(SENT, SEQS):
            total = total + factors[i] * kept[i - SENT, at]
        out_buf[at] = total.astype(jnp.bfloat16)
        copy(c).start()
        return carry

    lax.fori_loop(0, chunks, step, 0)
    for c in range(chunks):
        copy(c).wait()


def body(acts, out_grad, lengths):
    row = lax.axis_index("row")
    feats, width = acts.shape[1], out_grad.shape[1]
    devices = lax.axis_size("row") * lax.axis_size("col")
    act_full = lax.all_gather(acts, "col", axis=0, tiled=True)

    first = row * OWN
    slot = first % LEN + lax.broadcasted_iota(jnp.int32, (OWN, 1), 0)
    own = jnp.where(slot < lengths[first // LEN], out_grad, jnp.zeros_like(out_grad))
    left = z_ring(own[:, : width // 2])
    right = y_ring(own[:, width // 2 :])
    left = y_ring(jnp.concatenate(left, axis=0))
    right = z_ring(jnp.concatenate(right, axis=0))

    anywhere = pl.BlockSpec(memory_space=pl.ANY)
    vmem = pl.BlockSpec(memory_space=pltpu.VMEM)
    kept, sent, squares = pl.pallas_call(
        products_kernel,
        out_shape=(
            pltpu.VMEM((SEQS - SENT, feats, width), jnp.float32),
            jax.ShapeDtypeStruct((SEQS, feats, width), jnp.float32),
            jax.ShapeDtypeStruct((devices, SEQS), jnp.float32),
        ),
        in_specs=[anywhere] * 15,
        out_specs=(vmem, anywhere, vmem),
        scratch_shapes=[
            pltpu.VMEM((SEQS, LEN, width), jnp.bfloat16),
            pltpu.VMEM((2, LEN, feats), jnp.bfloat16),
            pltpu.VMEM((SENT, feats, width), jnp.float32),
            pltpu.SemaphoreType.DMA((NY,)),
            pltpu.SemaphoreType.DMA((2,)),
            pltpu.SemaphoreType.DMA((SENT,)),
        ],
        compiler_params=pltpu.CompilerParams(vmem_limit_bytes=32 << 20),
        name="sequence_products",
    )(act_full, *left, *right)
    parts = lax.all_to_all(squares, ("row", "col"), 0, 0, tiled=True)
    weight_grad, norms = pl.pallas_call(
        combine_kernel,
        out_shape=(
            jax.ShapeDtypeStruct((feats, width), jnp.bfloat16),
            jax.ShapeDtypeStruct((1, SEQS), jnp.float32),
        ),
        in_specs=[vmem, vmem, anywhere],
        out_specs=(anywhere, vmem),
        scratch_shapes=[
            pltpu.VMEM((feats, width), jnp.bfloat16),
            pltpu.VMEM((SENT, feats, width), jnp.float32),
            pltpu.SemaphoreType.DMA((feats // 128,)),
            pltpu.SemaphoreType.DMA((feats // 128,)),
        ],
        compiler_params=pltpu.CompilerParams(vmem_limit_bytes=16 << 20),
        name="scaled_sum",
    )(parts, kept, sent)
    return (weight_grad, norms.reshape(SEQS))


def solution(mesh):
    placed = (P("col", "row"), P("row", "col"), P())
    return jax.shard_map(
        body, mesh=mesh, in_specs=placed, out_specs=(P("row", "col"), P()), check_vma=False
    )
```
